256 devices in a mesh: tile: 64 (over x, y, z_lo, core), lev: 4 (over z_hi).
Axes of the slice: x: 4, y: 4, z: 8 (z_hi: 4, z_lo: 2; z = z_hi * 2 + z_lo), core: 2. Of those that a mesh axis runs over, the one named last changes fastest.
Arguments:
- adjoint_state: float32 [3, 16, 64, 128, 128], P(None, 'lev', 'tile'), may hold values from -6 to 6
- diffusivity: float32 [16, 64, 128, 128], P('lev', 'tile'), may hold values from 0.02 to 0.2
- retention: float32 [16, 64, 128, 128], P('lev', 'tile'), may hold values from 0 to 1, as said below
- coriolis: float32 [64, 128, 128], P('tile'), may hold values from -0.5 to 0.5
- neighbours: int32 [64, 4], replicated, may hold values from 0 to 63, as said below
- edge_from: int32 [64, 4], replicated, may hold values from 0 to 3
- rotation: int32 [64, 4], replicated, may hold values from 0 to 3
- seam_length: int32 [64, 4], replicated, may hold values from 32 to 128
- wet_mask: int32 [64, 128, 128], P('tile'), may hold values 0 or 1
Outputs:
- final_state: float32 [3, 16, 64, 128, 128], P(None, 'lev', 'tile')
The draws below stay inside these ranges and needn't reach their ends.
Inputs may be any that keep to these rules, and one draw needn't show every extreme that they name: The four neighbours of a tile are four different tiles, never the tile itself. `retention`: every entry lies strictly between 0 and 1.
All inputs are finite; a program needn't handle non-finite values. No bound on the sum of `wet_mask` on one device may be relied on, other than what follows from the above.
Results may differ from the reference program's by a relative error of at most 0.0003.
Values sent between devices are 32-bit elements; how exact they have to be, the bound alone decides.
A program may use at most 64 MiB of HBM per device.

```python
import math
import jax
import jax.numpy as jnp
from jax import lax

TILE_SIDE = 128
STEPS = 4
CUBE_TILES = 64
DEPTH_LEVELS = 16


def seam_tables(key):
    base = jax.random.fold_in(key, 11)
    first_key, second_key, tertiary_key = jax.random.split(base, 3)
    order = jax.random.permutation(first_key, CUBE_TILES).astype(jnp.int32)
    position = jnp.zeros((CUBE_TILES,), jnp.int32).at[order].set(jnp.arange(CUBE_TILES, dtype=jnp.int32))
    stride = max(CUBE_TILES // 4, 2)
    offsets = jnp.array([-1, 1, -stride, stride], jnp.int32)
    neighbour_table = order[(position[:, None] + offsets[None, :]) % CUBE_TILES]
    chosen = jax.random.randint(second_key, (CUBE_TILES, 4), 0, 4)
    turned = jax.random.randint(tertiary_key, (CUBE_TILES, 4), 1, 4)
    turn_table = jnp.where(chosen == 0, turned, 0).astype(jnp.int32)
    opposite = jnp.array([1, 0, 3, 2], jnp.int32)
    source_table = ((opposite[None, :] + turn_table) % 4).astype(jnp.int32)
    return (neighbour_table, source_table, turn_table)


def draw_neighbours(key, part):
    return seam_tables(key)[0]


def draw_edge_from(key, part):
    return seam_tables(key)[1]


def draw_rotation(key, part):
    return seam_tables(key)[2]


def draw_seam_length(key, part):
    raw = jax.random.randint(jax.random.fold_in(key, 23), (CUBE_TILES, 4), TILE_SIDE // 4, TILE_SIDE + TILE_SIDE // 2)
    return jnp.minimum(raw, TILE_SIDE).astype(jnp.int32)


def draw_retention(key, part):
    first_key, second_key, tertiary_key, quaternary_key = jax.random.split(jax.random.fold_in(key, 37), 4)
    low, high = (jnp.log(0.02), jnp.log(1.5))
    column_speed = jnp.exp(jax.random.uniform(first_key, (CUBE_TILES, TILE_SIDE, TILE_SIDE), jnp.float32, low, high))
    coarse_estimate = jax.random.uniform(second_key, (DEPTH_LEVELS, CUBE_TILES, TILE_SIDE, TILE_SIDE), jnp.float32, 0.7, 1.4)
    packet_cells = jax.random.uniform(tertiary_key, (DEPTH_LEVELS, CUBE_TILES, TILE_SIDE, TILE_SIDE), jnp.float32) < 1.0 / 12.0
    packet_size = jax.random.uniform(quaternary_key, (DEPTH_LEVELS, CUBE_TILES, TILE_SIDE, TILE_SIDE), jnp.float32, 0.5, 0.8)
    blend_weight = jnp.exp(-column_speed[None] * coarse_estimate) * jnp.where(packet_cells, packet_size, 1.0)
    return blend_weight.astype(jnp.float32)


def with_ends(values, own_key, least, largest):
    spot = [jax.random.randint(jax.random.fold_in(own_key, axis), (), 0, length) for axis, length in enumerate(values.shape)]
    longest = values.shape.index(max(values.shape))
    beside = spot[:longest] + [(spot[longest] + 1) % values.shape[longest]] + spot[longest + 1:]
    return values.at[tuple(spot)].set(least).at[tuple(beside)].set(largest)


def levels(own_key, shape, shards, low, top_value):
    def one(axis_at, parts):
        draws = jax.random.uniform(jax.random.fold_in(jax.random.fold_in(own_key, 6), axis_at), (parts,), jnp.float32, low / len(shards), top_value / len(shards))
        return jnp.repeat(jnp.exp(draws), shape[axis_at] // parts).reshape((-1,) + (1,) * (len(shape) - axis_at - 1))

    factor_of = one(*shards[0])
    for cut in shards[1:]:
        factor_of = factor_of * one(*cut)
    return factor_of


def normal_values(stream_key, shape, scale, bound, shards=(), kind=jnp.bfloat16):
    drawn = scale * jax.random.normal(stream_key, shape, jnp.float32)
    if shards:
        drawn = drawn * levels(stream_key, shape, shards, -0.22, 0.18)
    return jnp.clip(drawn, -bound, bound).astype(kind)


def setup_inputs(seed: int = 0) -> dict:
    streams_of = jax.random.split(jax.random.key(seed), 10)
    adjoint_state = normal_values(streams_of[0], (3, DEPTH_LEVELS, CUBE_TILES, TILE_SIDE, TILE_SIDE), 1.0, 6.0, ((1, 4), (2, 64)), jnp.float32)
    diffusivity = jnp.clip(jnp.exp(math.log(0.2) - 2.3025851 * jax.random.uniform(streams_of[1], (DEPTH_LEVELS, CUBE_TILES, TILE_SIDE, TILE_SIDE), jnp.float32) ** levels(streams_of[1], (DEPTH_LEVELS, CUBE_TILES, TILE_SIDE, TILE_SIDE), ((0, 4), (1, 64)), -0.2, 0.2)), 0.02, 0.2)
    retention = draw_retention(jax.random.fold_in(streams_of[9], 71), 0)
    coriolis = jnp.clip(jax.random.uniform(streams_of[3], (CUBE_TILES, TILE_SIDE, TILE_SIDE), jnp.float32, -0.5, 0.5) * levels(streams_of[3], (CUBE_TILES, TILE_SIDE, TILE_SIDE), ((0, 64),), -0.4, 0.0), -0.5, 0.5)
    neighbours = draw_neighbours(jax.random.fold_in(streams_of[9], 71), 0)
    edge_from = draw_edge_from(jax.random.fold_in(streams_of[9], 71), 0)
    rotation = draw_rotation(jax.random.fold_in(streams_of[9], 71), 0)
    seam_length = draw_seam_length(jax.random.fold_in(streams_of[9], 71), 0)
    wet_mask = with_ends((jax.random.randint(streams_of[8], (CUBE_TILES, TILE_SIDE, TILE_SIDE), 0, 8) < 7).astype(jnp.int32), jax.random.fold_in(streams_of[8], 1), 0, 1)
    return dict(adjoint_state=adjoint_state, diffusivity=diffusivity, retention=retention, coriolis=coriolis, neighbours=neighbours, edge_from=edge_from, rotation=rotation, seam_length=seam_length, wet_mask=wet_mask)


coupling = 0.25


def orient(strips, turns, seam_cells):
    size = strips.shape[-1]
    flipped = (turns == 1) | (turns == 2)
    strips = jnp.where(flipped, strips[..., ::-1], strips)
    cosine = (turns == 0).astype(jnp.float32) - (turns == 2).astype(jnp.float32)
    sine = (turns == 1).astype(jnp.float32) - (turns == 3).astype(jnp.float32)
    tracer = strips[0]
    zonal = strips[1]
    meridional = strips[2]
    new_zonal = cosine * zonal + sine * meridional
    new_meridional = cosine * meridional - sine * zonal
    inside = (lax.broadcasted_iota(jnp.int32, (size,), 0) < seam_cells).astype(jnp.float32)
    return jnp.stack([tracer * inside, new_zonal * inside, new_meridional * inside])


def edge_rows(state):
    return jnp.stack([state[..., :, 0], state[..., :, -1], state[..., 0, :], state[..., -1, :]], axis=-2)


def pad_with(state, halo_rows):
    widths = [(0, 0)] * (state.ndim - 2) + [(1, 1), (1, 1)]
    padded = jnp.pad(state, widths)
    padded = padded.at[..., 1:-1, 0].set(halo_rows[..., 0, :])
    padded = padded.at[..., 1:-1, -1].set(halo_rows[..., 1, :])
    padded = padded.at[..., 0, 1:-1].set(halo_rows[..., 2, :])
    padded = padded.at[..., -1, 1:-1].set(halo_rows[..., 3, :])
    return padded


def advance(padded, diffusivity, coriolis, wet_cells):
    centre = padded[..., 1:-1, 1:-1]
    east_side = padded[..., 1:-1, 2:]
    west_side = padded[..., 1:-1, :-2]
    north_side = padded[..., 2:, 1:-1]
    south_side = padded[..., :-2, 1:-1]
    laplacian = east_side + west_side + north_side + south_side - 4.0 * centre
    tracer = centre[0]
    zonal = centre[1]
    meridional = centre[2]
    new_tracer = tracer + diffusivity * laplacian[0] - coupling * 0.5 * ((east_side[1] - west_side[1]) + (north_side[2] - south_side[2]))
    new_zonal = zonal + diffusivity * laplacian[1] - coupling * 0.5 * (east_side[0] - west_side[0]) + coriolis * meridional
    new_meridional = meridional + diffusivity * laplacian[2] - coupling * 0.5 * (north_side[0] - south_side[0]) - coriolis * zonal
    return jnp.stack([new_tracer * wet_cells, new_zonal * wet_cells, new_meridional * wet_cells])


def settle(fresh, retention):
    def stepper(carry, inputs):
        values, blend_weight = inputs
        carry = (1.0 - blend_weight) * values + blend_weight * carry
        return carry, carry

    _, settled = lax.scan(stepper, jnp.zeros_like(fresh[:, 0]), (jnp.moveaxis(fresh, 1, 0), retention), reverse=True)
    return jnp.moveaxis(settled, 0, 1)


def reference(adjoint_state, diffusivity, retention, coriolis, neighbours, edge_from, rotation, seam_length, wet_mask):
    wet_cells = wet_mask.astype(jnp.float32)
    state = adjoint_state
    for step in range(STEPS):
        picked = edge_rows(state)[:, :, neighbours, edge_from, :]
        halo_rows = orient(picked, rotation[:, :, None], seam_length[:, :, None])
        fresh = advance(pad_with(state, halo_rows), diffusivity, coriolis, wet_cells)
        state = settle(fresh, retention)
    return state
```

```python
import functools

import jax
import jax.numpy as jnp
from jax import lax
from jax.experimental import pallas as pl
from jax.experimental.pallas import tpu as pltpu
from jax.sharding import PartitionSpec as P

STEPS = 4
COUPLING = 0.25
SIDE = 128
LEVELS = 4
PLANES = 3 * LEVELS
CHUNKS = 4
ROWS = SIDE // CHUNKS
SUB = 16
TOP = 8
MESH = pl.DeviceIdType.MESH
WEST, EAST, SOUTH, NORTH = range(4)


def distance(x, y):
    return min(x, 4 - x) + min(y, 4 - y)


PLANE = sorted(
    [(x, y, c) for x in range(4) for y in range(4) for c in range(2) if (x, y, c) != (0, 0, 0)],
    key=lambda d: (-distance(d[0], d[1]), -d[2]),
)
PEERS = len(PLANE)


def kernel(
    neighbours, edge_from, rotation, seam_length,
    state_hbm, diffusivity, retention, coriolis, wet_mask,
    out_hbm,
    state, wet, edges, packed, inner, halo, corner_up, corner_down,
    strip_mix, strip_keep, strip_spin, strip_wet,
    turn_cos, turn_sin, inside, flips,
    columns, chosen, sending, arrived, partner, gathered, theirs, carry_out, carry_in, strip_out, strip_in,
    load_sem, send_sem, arrive_sem, partner_send, partner_arrive,
    carry_send, carry_arrive, strip_send, strip_arrive,
):
    me = lax.axis_index("tile")
    lev = lax.axis_index("lev")
    px, py, pz, pc = me // 16, (me // 4) % 4, (me // 2) % 2, me % 2
    across = ((px * 4 + py) * 2 + (1 - pz)) * 2 + pc
    down, up = (lev + 3) % 4, (lev + 1) % 4
    half = COUPLING * 0.5

    def peer(d):
        return (((px + d[0]) % 4 * 4 + (py + d[1]) % 4) * 2 + pz) * 2 + (pc + d[2]) % 2

    load = pltpu.make_async_copy(state_hbm, state.at[0, :, :, pl.ds(TOP, SIDE)], load_sem)
    load.start()

    barrier = pltpu.get_barrier_semaphore()
    pl.semaphore_signal(barrier, inc=1, device_id={"tile": across}, device_id_type=MESH)
    for d in PLANE:
        pl.semaphore_signal(barrier, inc=1, device_id={"tile": peer(d)}, device_id_type=MESH)
    pl.semaphore_signal(barrier, inc=1, device_id={"lev": up}, device_id_type=MESH)
    pl.semaphore_signal(barrier, inc=1, device_id={"lev": down}, device_id_type=MESH)

    def choose(k, _):
        t = (k // 2) * 4 + pz * 2 + k % 2
        mine, theirs = jnp.int32(0), jnp.int32(0)
        for s in range(4):
            source, edge = neighbours[t, s], edge_from[t, s]
            mine = mine + jnp.where(source == me, edge, 0)
            theirs = theirs + jnp.where(source == across, edge, 0)
        chosen[0, t] = mine
        chosen[1, t] = theirs
        return 0

    lax.fori_loop(0, 32, choose, 0)

    lane4 = lax.broadcasted_iota(jnp.int32, (4, SIDE), 1)
    edge4 = lax.broadcasted_iota(jnp.int32, (4, SIDE), 0)
    lane_sub = lax.broadcasted_iota(jnp.int32, (ROWS, SIDE), 1)
    for s in range(4):
        turn = rotation[me, s]
        cells = seam_length[me, s]
        cosine = (turn == 0).astype(jnp.float32) - (turn == 2).astype(jnp.float32)
        sine = (turn == 1).astype(jnp.float32) - (turn == 3).astype(jnp.float32)
        flip = (turn == 1).astype(jnp.int32) + (turn == 2).astype(jnp.int32)
        within = jnp.where(lane4 < cells, 1.0, 0.0).astype(jnp.float32)
        inside[s] = within
        turn_cos[s] = within * cosine
        turn_sin[s] = within * sine
        flips[s] = jnp.zeros((4, SIDE), jnp.int32) + flip

    wet[...] = wet_mask[...].astype(jnp.float32)

    def transposed(read, count, first, last):
        for b in range(CHUNKS):
            found = jnp.zeros((ROWS, SIDE), jnp.float32)
            for p in range(count):
                value = pltpu.roll(read(p, b), (2 * p - first) % SIDE, 1)
                here = (lane_sub == 2 * p) | (lane_sub == (2 * p - first + last) % SIDE)
                found = jnp.where(here, value, found)
            columns[pl.ds(b * ROWS, ROWS), :] = found
        columns[...] = columns[...].T

    def row_of(p, first, last):
        return (2 * p - first + last) % SIDE

    def coefficient(p, b):
        rows = pl.ds(b * ROWS, ROWS)
        if p < LEVELS:
            return diffusivity[p, rows, :]
        if p < 2 * LEVELS:
            return retention[p - LEVELS, rows, :]
        return coriolis[rows, :] if p == 2 * LEVELS else wet[rows, :]

    transposed(coefficient, 2 * LEVELS + 2, 0, SIDE - 1)
    for p in range(2 * LEVELS + 2):
        if p < LEVELS:
            target, source = strip_mix.at[p], diffusivity.at[p]
        elif p < 2 * LEVELS:
            target, source = strip_keep.at[p - LEVELS], retention.at[p - LEVELS]
        else:
            target, source = (strip_spin, coriolis) if p == 2 * LEVELS else (strip_wet, wet)
        target[pl.ds(WEST, 1), :] = columns[pl.ds(2 * p, 1), :]
        target[pl.ds(EAST, 1), :] = columns[pl.ds(row_of(p, 0, SIDE - 1), 1), :]
        target[pl.ds(SOUTH, 1), :] = source[pl.ds(0, 1), :]
        target[pl.ds(NORTH, 1), :] = source[pl.ds(SIDE - 1, 1), :]

    load.wait()

    def plane_rows(now):
        return lambda p, b: state[now, p // LEVELS, p % LEVELS, pl.ds(TOP + b * ROWS, ROWS), :]

    transposed(plane_rows(0), PLANES, 0, SIDE - 1)
    for p in range(PLANES):
        c, l = p // LEVELS, p % LEVELS
        edges[c, l, pl.ds(WEST, 1), :] = columns[pl.ds(2 * p, 1), :]
        edges[c, l, pl.ds(EAST, 1), :] = columns[pl.ds(row_of(p, 0, SIDE - 1), 1), :]
        edges[c, l, pl.ds(SOUTH, 1), :] = state[0, c, l, pl.ds(TOP, 1), :]
        edges[c, l, pl.ds(NORTH, 1), :] = state[0, c, l, pl.ds(TOP + SIDE - 1, 1), :]
    for e in range(4):
        for c in range(3):
            packed[e, c] = edges[c, :, e, :]

    pl.semaphore_wait(barrier, PEERS + 3)

    def settle_edges(now):
        for p in range(PLANES):
            c, l = p // LEVELS, p % LEVELS
            columns[pl.ds(2 * p, 1), :] = edges[c, l, pl.ds(WEST, 1), :]
            columns[pl.ds(row_of(p, 0, SIDE - 1), 1), :] = edges[c, l, pl.ds(EAST, 1), :]
            state[now, c, l, pl.ds(TOP, 1), :] = edges[c, l, pl.ds(SOUTH, 1), :]
            state[now, c, l, pl.ds(TOP + SIDE - 1, 1), :] = edges[c, l, pl.ds(NORTH, 1), :]
        columns[...] = columns[...].T
        for b in range(CHUNKS):
            turned = columns[pl.ds(b * ROWS, ROWS), :]
            found = jnp.zeros((ROWS, SIDE), jnp.float32)
            for p in range(PLANES):
                c, l = p // LEVELS, p % LEVELS
                rows = pl.ds(TOP + b * ROWS, ROWS)
                rim = pltpu.roll(turned, (-2 * p) % SIDE, 1)
                value = jnp.where(
                    (lane_sub == 0) | (lane_sub == SIDE - 1), rim, state[now, c, l, rows, :]
                )
                state[now, c, l, rows, :] = value
                here = (lane_sub == 2 * p) | (lane_sub == row_of(p, 1, SIDE - 2))
                found = jnp.where(here, pltpu.roll(value, (2 * p - 1) % SIDE, 1), found)
            columns[pl.ds(b * ROWS, ROWS), :] = found
        columns[...] = columns[...].T
        for p in range(PLANES):
            c, l = p // LEVELS, p % LEVELS
            inner[c, l, pl.ds(WEST, 1), :] = columns[pl.ds(2 * p, 1), :]
            inner[c, l, pl.ds(EAST, 1), :] = columns[pl.ds(row_of(p, 1, SIDE - 2), 1), :]
            inner[c, l, pl.ds(SOUTH, 1), :] = state[now, c, l, pl.ds(TOP + 1, 1), :]
            inner[c, l, pl.ds(NORTH, 1), :] = state[now, c, l, pl.ds(TOP + SIDE - 2, 1), :]

    def carry_copy(r, j):
        return pltpu.make_async_remote_copy(
            carry_out.at[r, j], carry_in.at[r, j], carry_send.at[r, j], carry_arrive.at[r, j],
            device_id={"lev": down}, device_id_type=MESH,
        )

    def strip_copy(r):
        return pltpu.make_async_remote_copy(
            strip_out.at[r], strip_in.at[r], strip_send.at[r], strip_arrive.at[r],
            device_id={"lev": down}, device_id_type=MESH,
        )

    def partner_copy(r):
        return pltpu.make_async_remote_copy(
            packed, partner.at[r], partner_send.at[r], partner_arrive.at[r],
            device_id={"tile": across}, device_id_type=MESH,
        )

    def send(r, k, d, slot):
        pltpu.make_async_remote_copy(
            sending.at[k], arrived.at[r, slot], send_sem.at[r], arrive_sem.at[r],
            device_id={"tile": peer(d)}, device_id_type=MESH,
        ).start()

    def bulk(r, now, later, j):
        @pl.when(lev < 3)
        def _():
            carry_copy(r, j).wait_recv()

        for b in range(ROWS // SUB):
            at = j * ROWS + b * SUB
            cells = pl.ds(at, SUB)
            spin, dry = coriolis[cells, :], wet[cells, :]
            below = [
                jnp.where(lev == 3, 0.0, carry_in[r, j, c, pl.ds(b * SUB, SUB), :]) for c in range(3)
            ]
            for l in range(LEVELS - 1, -1, -1):
                mid = [state[now, c, l, pl.ds(TOP + at, SUB), :] for c in range(3)]
                north = [state[now, c, l, pl.ds(TOP + at + 1, SUB), :] for c in range(3)]
                south = [state[now, c, l, pl.ds(TOP + at - 1, SUB), :] for c in range(3)]
                east = [pltpu.roll(f, SIDE - 1, 1) for f in mid]
                west = [pltpu.roll(f, 1, 1) for f in mid]
                mix, keep = diffusivity[l, cells, :], retention[l, cells, :]
                spread = [
                    mid[c] + mix * (east[c] + west[c] + north[c] + south[c] - 4.0 * mid[c])
                    for c in range(3)
                ]
                fresh = [
                    spread[0] - half * ((east[1] - west[1]) + (north[2] - south[2])),
                    spread[1] - half * (east[0] - west[0]) + spin * mid[2],
                    spread[2] - half * (north[0] - south[0]) - spin * mid[1],
                ]
                open_keep = (1.0 - keep) * dry
                below = [open_keep * fresh[c] + keep * below[c] for c in range(3)]
                for c in range(3):
                    state[later, c, l, pl.ds(TOP + at, SUB), :] = below[c]
            for c in range(3):
                carry_out[r, j, c, pl.ds(b * SUB, SUB), :] = below[c]

        @pl.when(lev > 0)
        def _():
            carry_copy(r, j).start()

    def advance_edges(r):
        for s in range(4):
            source = neighbours[me, s]
            strip = gathered[source]
            turned = []
            for c in range(3):
                mirrored = jnp.take_along_axis(strip[c], SIDE - 1 - lane4, axis=1)
                turned.append(jnp.where(flips[s] > 0, mirrored, strip[c]))
            around = [
                turned[0] * inside[s],
                turn_cos[s] * turned[1] + turn_sin[s] * turned[2],
                turn_cos[s] * turned[2] - turn_sin[s] * turned[1],
            ]
            for c in range(3):
                halo[c, :, s, :] = around[c]
                if s == NORTH or s == EAST:
                    first = 0 if s == NORTH else 2
                    corner_up[c, :, first, :] = around[c]
                    corner_up[c, :, first + 1, :] = around[c]
                else:
                    first = 0 if s == SOUTH else 2
                    corner_down[c, :, first, :] = around[c]
                    corner_down[c, :, first + 1, :] = around[c]

        sides = edge4 < 2
        leading = (edge4 == WEST) | (edge4 == SOUTH)
        sign = jnp.where(leading, 1.0, -1.0).astype(jnp.float32)
        spin, dry = strip_spin[...], strip_wet[...]

        @pl.when(lev < 3)
        def _():
            strip_copy(r).wait_recv()

        below = [jnp.where(lev == 3, 0.0, strip_in[r, c]) for c in range(3)]
        for l in range(LEVELS - 1, -1, -1):
            mid = [edges[c, l] for c in range(3)]
            total, by_x, by_y = [], [], []
            for c in range(3):
                above, beneath = corner_up[c, l], corner_down[c, l]
                far = jnp.where(leading, pltpu.roll(above, SIDE - 1, 1), above)
                near = jnp.where(leading, beneath, pltpu.roll(beneath, 1, 1))
                ahead = jnp.where(lane4 == SIDE - 1, far, pltpu.roll(mid[c], SIDE - 1, 1))
                behind = jnp.where(lane4 == 0, near, pltpu.roll(mid[c], 1, 1))
                outer, within = halo[c, l], inner[c, l]
                total.append(outer + within + ahead + behind)
                through = sign * (within - outer)
                along = ahead - behind
                by_x.append(jnp.where(sides, through, along))
                by_y.append(jnp.where(sides, along, through))
            mix, keep = strip_mix[l], strip_keep[l]
            spread = [mid[c] + mix * (total[c] - 4.0 * mid[c]) for c in range(3)]
            fresh = [
                spread[0] - half * (by_x[1] + by_y[2]),
                spread[1] - half * by_x[0] + spin * mid[2],
                spread[2] - half * by_y[0] - spin * mid[1],
            ]
            open_keep = (1.0 - keep) * dry
            below = [open_keep * fresh[c] + keep * below[c] for c in range(3)]
            for c in range(3):
                edges[c, l] = below[c]
        for c in range(3):
            strip_out[r, c] = below[c]

        @pl.when(lev > 0)
        def _():
            strip_copy(r).start()

        for e in range(4):
            for c in range(3):
                packed[e, c] = edges[c, :, e, :]

    def step(r, _):
        now, later = r % 2, (r + 1) % 2
        partner_copy(r).start()
        for k, d in enumerate(PLANE):
            sending[k] = packed[chosen[0, peer(d)]]
            send(r, k, d, me)
        settle_edges(now)
        bulk(r, now, later, 0)
        partner_copy(r).wait()
        theirs[...] = partner[r]
        for k, d in enumerate(PLANE):
            sending[PEERS + k] = theirs[chosen[1, peer(d)]]
            send(r, PEERS + k, d, across)
        for j in range(1, CHUNKS):
            bulk(r, now, later, j)
        everyone = arrived.at[r, pl.ds(0, 2 * PEERS)]
        pltpu.make_async_remote_copy(
            everyone, everyone, send_sem.at[r], arrive_sem.at[r],
            device_id={"tile": across}, device_id_type=MESH,
        ).wait()
        gathered[...] = arrived[r]
        gathered[across] = theirs[chosen[1, me]]
        advance_edges(r)
        return 0

    lax.fori_loop(0, STEPS, step, 0)
    settle_edges(STEPS % 2)
    store = pltpu.make_async_copy(
        state.at[STEPS % 2, :, :, pl.ds(TOP, SIDE)], out_hbm, load_sem
    )
    store.start()

    @pl.when(lev > 0)
    def _():
        def drain(r, _):
            for j in range(CHUNKS):
                carry_copy(r, j).wait_send()
            strip_copy(r).wait_send()
            return 0

        lax.fori_loop(0, STEPS, drain, 0)

    store.wait()


def per_device(
    adjoint_state, diffusivity, retention, coriolis,
    neighbours, edge_from, rotation, seam_length, wet_mask,
):
    tiles = neighbours.shape[0]
    f32 = jnp.float32
    vmem, dma = pltpu.VMEM, pltpu.SemaphoreType.DMA
    strips = (3, LEVELS, 4, SIDE)
    small = pl.BlockSpec(memory_space=pltpu.SMEM)
    fast = pl.BlockSpec(memory_space=pltpu.VMEM)
    anywhere = pl.BlockSpec(memory_space=pl.ANY)
    out = pl.pallas_call(
        kernel,
        out_shape=jax.ShapeDtypeStruct((3, LEVELS, SIDE, SIDE), f32),
        in_specs=[small] * 4 + [anywhere] + [fast] * 4,
        out_specs=anywhere,
        scratch_shapes=[
            vmem((2, 3, LEVELS, SIDE + 2 * TOP, SIDE), f32),
            vmem((SIDE, SIDE), f32),
            vmem(strips, f32),
            vmem((4, 3, LEVELS, SIDE), f32),
            vmem(strips, f32),
            vmem(strips, f32),
            vmem(strips, f32),
            vmem(strips, f32),
            vmem((LEVELS, 4, SIDE), f32),
            vmem((LEVELS, 4, SIDE), f32),
            vmem((4, SIDE), f32),
            vmem((4, SIDE), f32),
            vmem((4, 4, SIDE), f32),
            vmem((4, 4, SIDE), f32),
            vmem((4, 4, SIDE), f32),
            vmem((4, 4, SIDE), jnp.int32),
            vmem((SIDE, SIDE), f32),
            pltpu.SMEM((2, tiles), jnp.int32),
            vmem((2 * PEERS, 3, LEVELS, SIDE), f32),
            vmem((STEPS, tiles, 3, LEVELS, SIDE), f32),
            vmem((STEPS, 4, 3, LEVELS, SIDE), f32),
            vmem((tiles, 3, LEVELS, SIDE), f32),
            vmem((4, 3, LEVELS, SIDE), f32),
            vmem((STEPS, CHUNKS, 3, ROWS, SIDE), f32),
            vmem((STEPS, CHUNKS, 3, ROWS, SIDE), f32),
            vmem((STEPS, 3, 4, SIDE), f32),
            vmem((STEPS, 3, 4, SIDE), f32),
            dma,
            dma((STEPS,)),
            dma((STEPS,)),
            dma((STEPS,)),
            dma((STEPS,)),
            dma((STEPS, CHUNKS)),
            dma((STEPS, CHUNKS)),
            dma((STEPS,)),
            dma((STEPS,)),
        ],
        compiler_params=pltpu.CompilerParams(
            collective_id=0, has_side_effects=True, vmem_limit_bytes=32 << 20
        ),
    )(
        neighbours, edge_from, rotation, seam_length,
        adjoint_state[:, :, 0], diffusivity[:, 0], retention[:, 0], coriolis[0], wet_mask[0],
    )
    return out[:, :, None]


def solution(mesh):
    in_specs = (
        P(None, "lev", "tile", None, None),
        P("lev", "tile", None, None),
        P("lev", "tile", None, None),
        P("tile", None, None),
        P(),
        P(),
        P(),
        P(),
        P("tile", None, None),
    )
    out_specs = P(None, "lev", "tile", None, None)
    return jax.shard_map(
        per_device, mesh=mesh, in_specs=in_specs, out_specs=out_specs, check_vma=False
    )
```

```python
import functools

import jax
import jax.numpy as jnp
from jax import lax
from jax.experimental import pallas as pl
from jax.experimental.pallas import tpu as pltpu
from jax.sharding import PartitionSpec as P

STEPS = 4
COUPLING = 0.25
SIDE = 128
LEVELS = 4
PLANES = 3 * LEVELS
CHUNKS = 4
FIRST = 1
EARLY = 4
ROWS = SIDE // CHUNKS
SUB = 16
TOP = 8
MESH = pl.DeviceIdType.MESH
WEST, EAST, SOUTH, NORTH = range(4)


def distance(x, y):
    return min(x, 4 - x) + min(y, 4 - y)


PLANE = sorted(
    [(x, y, c) for x in range(4) for y in range(4) for c in range(2) if (x, y, c) != (0, 0, 0)],
    key=lambda d: (-distance(d[0], d[1]), -d[2]),
)
PEERS = len(PLANE)


def kernel(
    neighbours, edge_from, rotation, seam_length,
    state_hbm, diffusivity_hbm, retention_hbm, coriolis_hbm, wet_hbm,
    out_hbm,
    state, diffusivity, retention, coriolis, wet_mask, wet, edges, packed, inner, halo, corner_up, corner_down,
    strip_mix, strip_keep, strip_spin, strip_wet,
    turn_cos, turn_sin, inside, flips,
    columns, chosen, sending, arrived, partner, gathered, theirs, carry_out, carry_in, strip_out, strip_in,
    load_sem, coefficient_sem, send_sem, arrive_sem, partner_send, partner_arrive,
    carry_send, carry_arrive, strip_send, strip_arrive,
):
    me = lax.axis_index("tile")
    lev = lax.axis_index("lev")
    px, py, pz, pc = me // 16, (me // 4) % 4, (me // 2) % 2, me % 2
    across = ((px * 4 + py) * 2 + (1 - pz)) * 2 + pc
    down, up = (lev + 3) % 4, (lev + 1) % 4
    half = COUPLING * 0.5

    def peer(d):
        return (((px + d[0]) % 4 * 4 + (py + d[1]) % 4) * 2 + pz) * 2 + (pc + d[2]) % 2

    load = pltpu.make_async_copy(state_hbm, state.at[0, :, :, pl.ds(TOP, SIDE)], load_sem)
    loads = [
        pltpu.make_async_copy(source, target, coefficient_sem.at[i])
        for i, (source, target) in enumerate(
            [
                (diffusivity_hbm, diffusivity), (retention_hbm, retention),
                (coriolis_hbm, coriolis), (wet_hbm, wet_mask),
            ]
        )
    ]
    for copy in loads:
        copy.start()
    load.start()

    barrier = pltpu.get_barrier_semaphore()
    pl.semaphore_signal(barrier, inc=1, device_id={"tile": across}, device_id_type=MESH)
    for d in PLANE:
        pl.semaphore_signal(barrier, inc=1, device_id={"tile": peer(d)}, device_id_type=MESH)
    pl.semaphore_signal(barrier, inc=1, device_id={"lev": up}, device_id_type=MESH)
    pl.semaphore_signal(barrier, inc=1, device_id={"lev": down}, device_id_type=MESH)

    def choose(k, _):
        t = (k // 2) * 4 + pz * 2 + k % 2
        mine, theirs = jnp.int32(0), jnp.int32(0)
        for s in range(4):
            source, edge = neighbours[s, t], edge_from[s, t]
            mine = mine + jnp.where(source == me, edge, 0)
            theirs = theirs + jnp.where(source == across, edge, 0)
        chosen[0, t] = mine
        chosen[1, t] = theirs
        return 0

    lax.fori_loop(0, 32, choose, 0)

    lane4 = lax.broadcasted_iota(jnp.int32, (4, SIDE), 1)
    edge4 = lax.broadcasted_iota(jnp.int32, (4, SIDE), 0)
    lane_sub = lax.broadcasted_iota(jnp.int32, (ROWS, SIDE), 1)
    for s in range(4):
        turn = rotation[s, me]
        cells = seam_length[s, me]
        cosine = (turn == 0).astype(jnp.float32) - (turn == 2).astype(jnp.float32)
        sine = (turn == 1).astype(jnp.float32) - (turn == 3).astype(jnp.float32)
        flip = (turn == 1).astype(jnp.int32) + (turn == 2).astype(jnp.int32)
        within = jnp.where(lane4 < cells, 1.0, 0.0).astype(jnp.float32)
        inside[s] = within
        turn_cos[s] = within * cosine
        turn_sin[s] = within * sine
        flips[s] = jnp.zeros((4, SIDE), jnp.int32) + flip

    for copy in loads:
        copy.wait()
    wet[...] = wet_mask[...].astype(jnp.float32)

    def transposed(read, count, first, last):
        for b in range(CHUNKS):
            found = jnp.zeros((ROWS, SIDE), jnp.float32)
            for p in range(count):
                value = pltpu.roll(read(p, b), (2 * p - first) % SIDE, 1)
                here = (lane_sub == 2 * p) | (lane_sub == (2 * p - first + last) % SIDE)
                found = jnp.where(here, value, found)
            columns[pl.ds(b * ROWS, ROWS), :] = found
        columns[...] = columns[...].T

    def row_of(p, first, last):
        return (2 * p - first + last) % SIDE

    def coefficient(p, b):
        rows = pl.ds(b * ROWS, ROWS)
        if p < LEVELS:
            return diffusivity[p, rows, :]
        if p < 2 * LEVELS:
            return retention[p - LEVELS, rows, :]
        return coriolis[rows, :] if p == 2 * LEVELS else wet[rows, :]

    transposed(coefficient, 2 * LEVELS + 2, 0, SIDE - 1)
    for p in range(2 * LEVELS + 2):
        if p < LEVELS:
            target, source = strip_mix.at[p], diffusivity.at[p]
        elif p < 2 * LEVELS:
            target, source = strip_keep.at[p - LEVELS], retention.at[p - LEVELS]
        else:
            target, source = (strip_spin, coriolis) if p == 2 * LEVELS else (strip_wet, wet)
        target[pl.ds(WEST, 1), :] = columns[pl.ds(2 * p, 1), :]
        target[pl.ds(EAST, 1), :] = columns[pl.ds(row_of(p, 0, SIDE - 1), 1), :]
        target[pl.ds(SOUTH, 1), :] = source[pl.ds(0, 1), :]
        target[pl.ds(NORTH, 1), :] = source[pl.ds(SIDE - 1, 1), :]

    load.wait()

    def plane_rows(now):
        return lambda p, b: state[now, p // LEVELS, p % LEVELS, pl.ds(TOP + b * ROWS, ROWS), :]

    transposed(plane_rows(0), PLANES, 0, SIDE - 1)
    for p in range(PLANES):
        c, l = p // LEVELS, p % LEVELS
        edges[c, l, pl.ds(WEST, 1), :] = columns[pl.ds(2 * p, 1), :]
        edges[c, l, pl.ds(EAST, 1), :] = columns[pl.ds(row_of(p, 0, SIDE - 1), 1), :]
        edges[c, l, pl.ds(SOUTH, 1), :] = state[0, c, l, pl.ds(TOP, 1), :]
        edges[c, l, pl.ds(NORTH, 1), :] = state[0, c, l, pl.ds(TOP + SIDE - 1, 1), :]
    for e in range(4):
        for c in range(3):
            packed[e, c] = edges[c, :, e, :]

    pl.semaphore_wait(barrier, PEERS + 3)

    def settle_edges(now):
        for p in range(PLANES):
            c, l = p // LEVELS, p % LEVELS
            columns[pl.ds(2 * p, 1), :] = edges[c, l, pl.ds(WEST, 1), :]
            columns[pl.ds(row_of(p, 0, SIDE - 1), 1), :] = edges[c, l, pl.ds(EAST, 1), :]
            state[now, c, l, pl.ds(TOP, 1), :] = edges[c, l, pl.ds(SOUTH, 1), :]
            state[now, c, l, pl.ds(TOP + SIDE - 1, 1), :] = edges[c, l, pl.ds(NORTH, 1), :]
        columns[...] = columns[...].T
        for b in range(CHUNKS):
            turned = columns[pl.ds(b * ROWS, ROWS), :]
            found = jnp.zeros((ROWS, SIDE), jnp.float32)
            for p in range(PLANES):
                c, l = p // LEVELS, p % LEVELS
                rows = pl.ds(TOP + b * ROWS, ROWS)
                rim = pltpu.roll(turned, (-2 * p) % SIDE, 1)
                value = jnp.where(
                    (lane_sub == 0) | (lane_sub == SIDE - 1), rim, state[now, c, l, rows, :]
                )
                state[now, c, l, rows, :] = value
                here = (lane_sub == 2 * p) | (lane_sub == row_of(p, 1, SIDE - 2))
                found = jnp.where(here, pltpu.roll(value, (2 * p - 1) % SIDE, 1), found)
            columns[pl.ds(b * ROWS, ROWS), :] = found
        columns[...] = columns[...].T
        for p in range(PLANES):
            c, l = p // LEVELS, p % LEVELS
            inner[c, l, pl.ds(WEST, 1), :] = columns[pl.ds(2 * p, 1), :]
            inner[c, l, pl.ds(EAST, 1), :] = columns[pl.ds(row_of(p, 1, SIDE - 2), 1), :]
            inner[c, l, pl.ds(SOUTH, 1), :] = state[now, c, l, pl.ds(TOP + 1, 1), :]
            inner[c, l, pl.ds(NORTH, 1), :] = state[now, c, l, pl.ds(TOP + SIDE - 2, 1), :]

    def carry_copy(r, j):
        return pltpu.make_async_remote_copy(
            carry_out.at[r, j], carry_in.at[r, j], carry_send.at[r, j], carry_arrive.at[r, j],
            device_id={"lev": down}, device_id_type=MESH,
        )

    def strip_copy(r):
        return pltpu.make_async_remote_copy(
            strip_out.at[r], strip_in.at[r], strip_send.at[r], strip_arrive.at[r],
            device_id={"lev": down}, device_id_type=MESH,
        )

    def partner_copy(r):
        return pltpu.make_async_remote_copy(
            packed, partner.at[r], partner_send.at[r], partner_arrive.at[r],
            device_id={"tile": across}, device_id_type=MESH,
        )

    def send(r, k, d, slot):
        pltpu.make_async_remote_copy(
            sending.at[k], arrived.at[r, slot], send_sem.at[r], arrive_sem.at[r],
            device_id={"tile": peer(d)}, device_id_type=MESH,
        ).start()

    def bulk(r, j):
        now, later = r % 2, (r + 1) % 2

        @pl.when(lev < 3)
        def _():
            carry_copy(r, j).wait_recv()

        for b in range(ROWS // SUB):
            at = j * ROWS + b * SUB
            cells = pl.ds(at, SUB)
            spin, dry = coriolis[cells, :], wet[cells, :]
            below = [
                jnp.where(lev == 3, 0.0, carry_in[r, j, c, pl.ds(b * SUB, SUB), :]) for c in range(3)
            ]
            for l in range(LEVELS - 1, -1, -1):
                mid = [state[now, c, l, pl.ds(TOP + at, SUB), :] for c in range(3)]
                north = [state[now, c, l, pl.ds(TOP + at + 1, SUB), :] for c in range(3)]
                south = [state[now, c, l, pl.ds(TOP + at - 1, SUB), :] for c in range(3)]
                east = [pltpu.roll(f, SIDE - 1, 1) for f in mid]
                west = [pltpu.roll(f, 1, 1) for f in mid]
                mix, keep = diffusivity[l, cells, :], retention[l, cells, :]
                spread = [
                    mid[c] + mix * (east[c] + west[c] + north[c] + south[c] - 4.0 * mid[c])
                    for c in range(3)
                ]
                fresh = [
                    spread[0] - half * ((east[1] - west[1]) + (north[2] - south[2])),
                    spread[1] - half * (east[0] - west[0]) + spin * mid[2],
                    spread[2] - half * (north[0] - south[0]) - spin * mid[1],
                ]
                open_keep = (1.0 - keep) * dry
                below = [open_keep * fresh[c] + keep * below[c] for c in range(3)]
                for c in range(3):
                    state[later, c, l, pl.ds(TOP + at, SUB), :] = below[c]
            for c in range(3):
                carry_out[r, j, c, pl.ds(b * SUB, SUB), :] = below[c]

        @pl.when(lev > 0)
        def _():
            carry_copy(r, j).start()

    def advance_edges(r):
        for s in range(4):
            source = neighbours[s, me]
            strip = gathered[source]
            turned = []
            for c in range(3):
                mirrored = jnp.take_along_axis(strip[c], SIDE - 1 - lane4, axis=1)
                turned.append(jnp.where(flips[s] > 0, mirrored, strip[c]))
            around = [
                turned[0] * inside[s],
                turn_cos[s] * turned[1] + turn_sin[s] * turned[2],
                turn_cos[s] * turned[2] - turn_sin[s] * turned[1],
            ]
            for c in range(3):
                halo[c, :, s, :] = around[c]
                if s == NORTH or s == EAST:
                    first = 0 if s == NORTH else 2
                    corner_up[c, :, first, :] = around[c]
                    corner_up[c, :, first + 1, :] = around[c]
                else:
                    first = 0 if s == SOUTH else 2
                    corner_down[c, :, first, :] = around[c]
                    corner_down[c, :, first + 1, :] = around[c]

        sides = edge4 < 2
        leading = (edge4 == WEST) | (edge4 == SOUTH)
        sign = jnp.where(leading, 1.0, -1.0).astype(jnp.float32)
        spin, dry = strip_spin[...], strip_wet[...]

        grown = [None] * LEVELS
        for l in range(LEVELS - 1, -1, -1):
            mid = [edges[c, l] for c in range(3)]
            total, by_x, by_y = [], [], []
            for c in range(3):
                above, beneath = corner_up[c, l], corner_down[c, l]
                far = jnp.where(leading, pltpu.roll(above, SIDE - 1, 1), above)
                near = jnp.where(leading, beneath, pltpu.roll(beneath, 1, 1))
                ahead = jnp.where(lane4 == SIDE - 1, far, pltpu.roll(mid[c], SIDE - 1, 1))
                behind = jnp.where(lane4 == 0, near, pltpu.roll(mid[c], 1, 1))
                outer, within = halo[c, l], inner[c, l]
                total.append(outer + within + ahead + behind)
                through = sign * (within - outer)
                along = ahead - behind
                by_x.append(jnp.where(sides, through, along))
                by_y.append(jnp.where(sides, along, through))
            mix, keep = strip_mix[l], strip_keep[l]
            spread = [mid[c] + mix * (total[c] - 4.0 * mid[c]) for c in range(3)]
            fresh = [
                spread[0] - half * (by_x[1] + by_y[2]),
                spread[1] - half * by_x[0] + spin * mid[2],
                spread[2] - half * by_y[0] - spin * mid[1],
            ]
            open_keep = (1.0 - keep) * dry
            grown[l] = [open_keep * fresh[c] for c in range(3)]

        @pl.when(lev < 3)
        def _():
            strip_copy(r).wait_recv()

        below = [jnp.where(lev == 3, 0.0, strip_in[r, c]) for c in range(3)]
        for l in range(LEVELS - 1, -1, -1):
            below = [grown[l][c] + strip_keep[l] * below[c] for c in range(3)]
            for c in range(3):
                edges[c, l] = below[c]
        for c in range(3):
            strip_out[r, c] = below[c]

        @pl.when(lev > 0)
        def _():
            strip_copy(r).start()

        for e in range(4):
            for c in range(3):
                packed[e, c] = edges[c, :, e, :]

    def step(r, _):
        partner_copy(r).start()
        for k, d in enumerate(PLANE):
            sending[k] = packed[chosen[0, peer(d)]]
            send(r, k, d, me)

        @pl.when(r > 0)
        def _():
            for j in range(EARLY, CHUNKS):
                bulk(r - 1, j)

        settle_edges(r % 2)
        for j in range(FIRST):
            bulk(r, j)
        partner_copy(r).wait()
        theirs[...] = partner[r]
        for k, d in enumerate(PLANE):
            sending[PEERS + k] = theirs[chosen[1, peer(d)]]
            send(r, PEERS + k, d, across)
        for j in range(FIRST, EARLY):
            bulk(r, j)
        everyone = arrived.at[r, pl.ds(0, 2 * PEERS)]
        pltpu.make_async_remote_copy(
            everyone, everyone, send_sem.at[r], arrive_sem.at[r],
            device_id={"tile": across}, device_id_type=MESH,
        ).wait()
        gathered[...] = arrived[r]
        gathered[across] = theirs[chosen[1, me]]
        advance_edges(r)
        return 0

    lax.fori_loop(0, STEPS, step, 0)
    for j in range(EARLY, CHUNKS):
        bulk(STEPS - 1, j)
    settle_edges(STEPS % 2)
    store = pltpu.make_async_copy(
        state.at[STEPS % 2, :, :, pl.ds(TOP, SIDE)], out_hbm, load_sem
    )
    store.start()

    @pl.when(lev > 0)
    def _():
        def drain(r, _):
            for j in range(CHUNKS):
                carry_copy(r, j).wait_send()
            strip_copy(r).wait_send()
            return 0

        lax.fori_loop(0, STEPS, drain, 0)

    store.wait()


def per_device(
    adjoint_state, diffusivity, retention, coriolis,
    neighbours, edge_from, rotation, seam_length, wet_mask,
):
    tiles = neighbours.shape[0]
    f32 = jnp.float32
    vmem, dma = pltpu.VMEM, pltpu.SemaphoreType.DMA
    strips = (3, LEVELS, 4, SIDE)
    small = pl.BlockSpec(memory_space=pltpu.SMEM)
    anywhere = pl.BlockSpec(memory_space=pltpu.HBM)
    out = pl.pallas_call(
        kernel,
        out_shape=jax.ShapeDtypeStruct((3, LEVELS, SIDE, SIDE), f32),
        in_specs=[small] * 4 + [anywhere] * 5,
        out_specs=pl.BlockSpec(memory_space=pltpu.VMEM),
        scratch_shapes=[
            vmem((2, 3, LEVELS, SIDE + 2 * TOP, SIDE), f32),
            vmem((LEVELS, SIDE, SIDE), f32),
            vmem((LEVELS, SIDE, SIDE), f32),
            vmem((SIDE, SIDE), f32),
            vmem((SIDE, SIDE), jnp.int32),
            vmem((SIDE, SIDE), f32),
            vmem(strips, f32),
            vmem((4, 3, LEVELS, SIDE), f32),
            vmem(strips, f32),
            vmem(strips, f32),
            vmem(strips, f32),
            vmem(strips, f32),
            vmem((LEVELS, 4, SIDE), f32),
            vmem((LEVELS, 4, SIDE), f32),
            vmem((4, SIDE), f32),
            vmem((4, SIDE), f32),
            vmem((4, 4, SIDE), f32),
            vmem((4, 4, SIDE), f32),
            vmem((4, 4, SIDE), f32),
            vmem((4, 4, SIDE), jnp.int32),
            vmem((SIDE, SIDE), f32),
            pltpu.SMEM((2, tiles), jnp.int32),
            vmem((2 * PEERS, 3, LEVELS, SIDE), f32),
            vmem((STEPS, tiles, 3, LEVELS, SIDE), f32),
            vmem((STEPS, 4, 3, LEVELS, SIDE), f32),
            vmem((tiles, 3, LEVELS, SIDE), f32),
            vmem((4, 3, LEVELS, SIDE), f32),
            vmem((STEPS, CHUNKS, 3, ROWS, SIDE), f32),
            vmem((STEPS, CHUNKS, 3, ROWS, SIDE), f32),
            vmem((STEPS, 3, 4, SIDE), f32),
            vmem((STEPS, 3, 4, SIDE), f32),
            dma,
            dma((4,)),
            dma((STEPS,)),
            dma((STEPS,)),
            dma((STEPS,)),
            dma((STEPS,)),
            dma((STEPS, CHUNKS)),
            dma((STEPS, CHUNKS)),
            dma((STEPS,)),
            dma((STEPS,)),
        ],
        compiler_params=pltpu.CompilerParams(
            collective_id=0, has_side_effects=True, vmem_limit_bytes=60 << 20
        ),
    )(
        neighbours.T, edge_from.T, rotation.T, seam_length.T,
        adjoint_state[:, :, 0], diffusivity[:, 0], retention[:, 0], coriolis[0], wet_mask[0],
    )
    return out[:, :, None]


def solution(mesh):
    in_specs = (
        P(None, "lev", "tile", None, None),
        P("lev", "tile", None, None),
        P("lev", "tile", None, None),
        P("tile", None, None),
        P(),
        P(),
        P(),
        P(),
        P("tile", None, None),
    )
    out_specs = P(None, "lev", "tile", None, None)
    return jax.shard_map(
        per_device, mesh=mesh, in_specs=in_specs, out_specs=out_specs, check_vma=False
    )
```

```python
import functools

import jax
import jax.numpy as jnp
from jax import lax
from jax.experimental import pallas as pl
from jax.experimental.pallas import tpu as pltpu
from jax.sharding import PartitionSpec as P

STEPS = 4
COUPLING = 0.25
SIDE = 128
LEVELS = 4
PLANES = 3 * LEVELS
CHUNKS = 8
FIRST = 2
EARLY = 8
ROWS = SIDE // CHUNKS
SUB = 16
TOP = 8
MESH = pl.DeviceIdType.MESH
WEST, EAST, SOUTH, NORTH = range(4)


def distance(x, y):
    return min(x, 4 - x) + min(y, 4 - y)


PLANE = sorted(
    [(x, y, c) for x in range(4) for y in range(4) for c in range(2) if (x, y, c) != (0, 0, 0)],
    key=lambda d: (-distance(d[0], d[1]), -d[2]),
)
PEERS = len(PLANE)


def kernel(
    neighbours, edge_from, rotation, seam_length,
    state_hbm, diffusivity_hbm, retention_hbm, coriolis_hbm, wet_hbm,
    out_hbm,
    state, diffusivity, retention, coriolis, wet_mask, wet, edges, packed, inner, halo, corner_up, corner_down,
    strip_mix, strip_keep, strip_spin, strip_wet,
    turn_cos, turn_sin, inside, flips,
    columns, chosen, sending, arrived, partner, gathered, theirs, carry_out, carry_in, strip_out, strip_in,
    load_sem, coefficient_sem, send_sem, arrive_sem, partner_send, partner_arrive,
    carry_send, carry_arrive, strip_send, strip_arrive,
):
    me = lax.axis_index("tile")
    lev = lax.axis_index("lev")
    px, py, pz, pc = me // 16, (me // 4) % 4, (me // 2) % 2, me % 2
    across = ((px * 4 + py) * 2 + (1 - pz)) * 2 + pc
    down, up = (lev + 3) % 4, (lev + 1) % 4
    half = COUPLING * 0.5

    def peer(d):
        return (((px + d[0]) % 4 * 4 + (py + d[1]) % 4) * 2 + pz) * 2 + (pc + d[2]) % 2

    load = pltpu.make_async_copy(state_hbm, state.at[0, :, :, pl.ds(TOP, SIDE)], load_sem)
    loads = [
        pltpu.make_async_copy(source, target, coefficient_sem.at[i])
        for i, (source, target) in enumerate(
            [
                (diffusivity_hbm, diffusivity), (retention_hbm, retention),
                (coriolis_hbm, coriolis), (wet_hbm, wet_mask),
            ]
        )
    ]
    for copy in loads:
        copy.start()
    load.start()

    barrier = pltpu.get_barrier_semaphore()
    pl.semaphore_signal(barrier, inc=1, device_id={"tile": across}, device_id_type=MESH)
    for d in PLANE:
        pl.semaphore_signal(barrier, inc=1, device_id={"tile": peer(d)}, device_id_type=MESH)
    pl.semaphore_signal(barrier, inc=1, device_id={"lev": up}, device_id_type=MESH)
    pl.semaphore_signal(barrier, inc=1, device_id={"lev": down}, device_id_type=MESH)

    def choose(k, _):
        t = (k // 2) * 4 + pz * 2 + k % 2
        mine, theirs = jnp.int32(0), jnp.int32(0)
        for s in range(4):
            source, edge = neighbours[s, t], edge_from[s, t]
            mine = mine + jnp.where(source == me, edge, 0)
            theirs = theirs + jnp.where(source == across, edge, 0)
        chosen[0, t] = mine
        chosen[1, t] = theirs
        return 0

    lax.fori_loop(0, 32, choose, 0)

    lane4 = lax.broadcasted_iota(jnp.int32, (4, SIDE), 1)
    edge4 = lax.broadcasted_iota(jnp.int32, (4, SIDE), 0)
    lane_sub = lax.broadcasted_iota(jnp.int32, (ROWS, SIDE), 1)
    for s in range(4):
        turn = rotation[s, me]
        cells = seam_length[s, me]
        cosine = (turn == 0).astype(jnp.float32) - (turn == 2).astype(jnp.float32)
        sine = (turn == 1).astype(jnp.float32) - (turn == 3).astype(jnp.float32)
        flip = (turn == 1).astype(jnp.int32) + (turn == 2).astype(jnp.int32)
        within = jnp.where(lane4 < cells, 1.0, 0.0).astype(jnp.float32)
        inside[s] = within
        turn_cos[s] = within * cosine
        turn_sin[s] = within * sine
        flips[s] = jnp.zeros((4, SIDE), jnp.int32) + flip

    for copy in loads:
        copy.wait()
    wet[...] = wet_mask[...].astype(jnp.float32)

    def transposed(read, count, first, last):
        for b in range(CHUNKS):
            found = jnp.zeros((ROWS, SIDE), jnp.float32)
            for p in range(count):
                value = pltpu.roll(read(p, b), (2 * p - first) % SIDE, 1)
                here = (lane_sub == 2 * p) | (lane_sub == (2 * p - first + last) % SIDE)
                found = jnp.where(here, value, found)
            columns[pl.ds(b * ROWS, ROWS), :] = found
        columns[...] = columns[...].T

    def row_of(p, first, last):
        return (2 * p - first + last) % SIDE

    def coefficient(p, b):
        rows = pl.ds(b * ROWS, ROWS)
        if p < LEVELS:
            return diffusivity[p, rows, :]
        if p < 2 * LEVELS:
            return retention[p - LEVELS, rows, :]
        return coriolis[rows, :] if p == 2 * LEVELS else wet[rows, :]

    transposed(coefficient, 2 * LEVELS + 2, 0, SIDE - 1)
    for p in range(2 * LEVELS + 2):
        if p < LEVELS:
            target, source = strip_mix.at[p], diffusivity.at[p]
        elif p < 2 * LEVELS:
            target, source = strip_keep.at[p - LEVELS], retention.at[p - LEVELS]
        else:
            target, source = (strip_spin, coriolis) if p == 2 * LEVELS else (strip_wet, wet)
        target[pl.ds(WEST, 1), :] = columns[pl.ds(2 * p, 1), :]
        target[pl.ds(EAST, 1), :] = columns[pl.ds(row_of(p, 0, SIDE - 1), 1), :]
        target[pl.ds(SOUTH, 1), :] = source[pl.ds(0, 1), :]
        target[pl.ds(NORTH, 1), :] = source[pl.ds(SIDE - 1, 1), :]

    load.wait()

    def plane_rows(now):
        return lambda p, b: state[now, p // LEVELS, p % LEVELS, pl.ds(TOP + b * ROWS, ROWS), :]

    transposed(plane_rows(0), PLANES, 0, SIDE - 1)
    for p in range(PLANES):
        c, l = p // LEVELS, p % LEVELS
        edges[c, l, pl.ds(WEST, 1), :] = columns[pl.ds(2 * p, 1), :]
        edges[c, l, pl.ds(EAST, 1), :] = columns[pl.ds(row_of(p, 0, SIDE - 1), 1), :]
        edges[c, l, pl.ds(SOUTH, 1), :] = state[0, c, l, pl.ds(TOP, 1), :]
        edges[c, l, pl.ds(NORTH, 1), :] = state[0, c, l, pl.ds(TOP + SIDE - 1, 1), :]
    for e in range(4):
        for c in range(3):
            packed[e, c] = edges[c, :, e, :]

    pl.semaphore_wait(barrier, PEERS + 3)

    def settle_edges(now):
        for p in range(PLANES):
            c, l = p // LEVELS, p % LEVELS
            columns[pl.ds(2 * p, 1), :] = edges[c, l, pl.ds(WEST, 1), :]
            columns[pl.ds(row_of(p, 0, SIDE - 1), 1), :] = edges[c, l, pl.ds(EAST, 1), :]
            state[now, c, l, pl.ds(TOP, 1), :] = edges[c, l, pl.ds(SOUTH, 1), :]
            state[now, c, l, pl.ds(TOP + SIDE - 1, 1), :] = edges[c, l, pl.ds(NORTH, 1), :]
        columns[...] = columns[...].T
        for b in range(CHUNKS):
            turned = columns[pl.ds(b * ROWS, ROWS), :]
            found = jnp.zeros((ROWS, SIDE), jnp.float32)
            for p in range(PLANES):
                c, l = p // LEVELS, p % LEVELS
                rows = pl.ds(TOP + b * ROWS, ROWS)
                rim = pltpu.roll(turned, (-2 * p) % SIDE, 1)
                value = jnp.where(
                    (lane_sub == 0) | (lane_sub == SIDE - 1), rim, state[now, c, l, rows, :]
                )
                state[now, c, l, rows, :] = value
                here = (lane_sub == 2 * p) | (lane_sub == row_of(p, 1, SIDE - 2))
                found = jnp.where(here, pltpu.roll(value, (2 * p - 1) % SIDE, 1), found)
            columns[pl.ds(b * ROWS, ROWS), :] = found
        columns[...] = columns[...].T
        for p in range(PLANES):
            c, l = p // LEVELS, p % LEVELS
            inner[c, l, pl.ds(WEST, 1), :] = columns[pl.ds(2 * p, 1), :]
            inner[c, l, pl.ds(EAST, 1), :] = columns[pl.ds(row_of(p, 1, SIDE - 2), 1), :]
            inner[c, l, pl.ds(SOUTH, 1), :] = state[now, c, l, pl.ds(TOP + 1, 1), :]
            inner[c, l, pl.ds(NORTH, 1), :] = state[now, c, l, pl.ds(TOP + SIDE - 2, 1), :]

    def carry_copy(r, j):
        return pltpu.make_async_remote_copy(
            carry_out.at[r, j], carry_in.at[r, j], carry_send.at[r, j], carry_arrive.at[r, j],
            device_id={"lev": down}, device_id_type=MESH,
        )

    def strip_copy(r):
        return pltpu.make_async_remote_copy(
            strip_out.at[r], strip_in.at[r], strip_send.at[r], strip_arrive.at[r],
            device_id={"lev": down}, device_id_type=MESH,
        )

    def partner_copy(r):
        return pltpu.make_async_remote_copy(
            packed, partner.at[r], partner_send.at[r], partner_arrive.at[r],
            device_id={"tile": across}, device_id_type=MESH,
        )

    def send(r, k, d, slot):
        pltpu.make_async_remote_copy(
            sending.at[k], arrived.at[r, slot], send_sem.at[r], arrive_sem.at[r],
            device_id={"tile": peer(d)}, device_id_type=MESH,
        ).start()

    def bulk(r, j):
        now, later = r % 2, (r + 1) % 2

        @pl.when(lev < 3)
        def _():
            carry_copy(r, j).wait_recv()

        for b in range(ROWS // SUB):
            at = j * ROWS + b * SUB
            cells = pl.ds(at, SUB)
            spin, dry = coriolis[cells, :], wet[cells, :]
            below = [
                jnp.where(lev == 3, 0.0, carry_in[r, j, c, pl.ds(b * SUB, SUB), :]) for c in range(3)
            ]
            for l in range(LEVELS - 1, -1, -1):
                mid = [state[now, c, l, pl.ds(TOP + at, SUB), :] for c in range(3)]
                north = [state[now, c, l, pl.ds(TOP + at + 1, SUB), :] for c in range(3)]
                south = [state[now, c, l, pl.ds(TOP + at - 1, SUB), :] for c in range(3)]
                east = [pltpu.roll(f, SIDE - 1, 1) for f in mid]
                west = [pltpu.roll(f, 1, 1) for f in mid]
                mix, keep = diffusivity[l, cells, :], retention[l, cells, :]
                spread = [
                    mid[c] + mix * (east[c] + west[c] + north[c] + south[c] - 4.0 * mid[c])
                    for c in range(3)
                ]
                fresh = [
                    spread[0] - half * ((east[1] - west[1]) + (north[2] - south[2])),
                    spread[1] - half * (east[0] - west[0]) + spin * mid[2],
                    spread[2] - half * (north[0] - south[0]) - spin * mid[1],
                ]
                open_keep = (1.0 - keep) * dry
                below = [open_keep * fresh[c] + keep * below[c] for c in range(3)]
                for c in range(3):
                    state[later, c, l, pl.ds(TOP + at, SUB), :] = below[c]
            for c in range(3):
                carry_out[r, j, c, pl.ds(b * SUB, SUB), :] = below[c]

        @pl.when(lev > 0)
        def _():
            if j >= 2:
                carry_copy(r, j - 2).wait_send()
            carry_copy(r, j).start()

    def advance_edges(r):
        for s in range(4):
            source = neighbours[s, me]
            strip = gathered[source]
            turned = []
            for c in range(3):
                mirrored = jnp.take_along_axis(strip[c], SIDE - 1 - lane4, axis=1)
                turned.append(jnp.where(flips[s] > 0, mirrored, strip[c]))
            around = [
                turned[0] * inside[s],
                turn_cos[s] * turned[1] + turn_sin[s] * turned[2],
                turn_cos[s] * turned[2] - turn_sin[s] * turned[1],
            ]
            for c in range(3):
                halo[c, :, s, :] = around[c]
                if s == NORTH or s == EAST:
                    first = 0 if s == NORTH else 2
                    corner_up[c, :, first, :] = around[c]
                    corner_up[c, :, first + 1, :] = around[c]
                else:
                    first = 0 if s == SOUTH else 2
                    corner_down[c, :, first, :] = around[c]
                    corner_down[c, :, first + 1, :] = around[c]

        sides = edge4 < 2
        leading = (edge4 == WEST) | (edge4 == SOUTH)
        sign = jnp.where(leading, 1.0, -1.0).astype(jnp.float32)
        spin, dry = strip_spin[...], strip_wet[...]

        grown = [None] * LEVELS
        for l in range(LEVELS - 1, -1, -1):
            mid = [edges[c, l] for c in range(3)]
            total, by_x, by_y = [], [], []
            for c in range(3):
                above, beneath = corner_up[c, l], corner_down[c, l]
                far = jnp.where(leading, pltpu.roll(above, SIDE - 1, 1), above)
                near = jnp.where(leading, beneath, pltpu.roll(beneath, 1, 1))
                ahead = jnp.where(lane4 == SIDE - 1, far, pltpu.roll(mid[c], SIDE - 1, 1))
                behind = jnp.where(lane4 == 0, near, pltpu.roll(mid[c], 1, 1))
                outer, within = halo[c, l], inner[c, l]
                total.append(outer + within + ahead + behind)
                through = sign * (within - outer)
                along = ahead - behind
                by_x.append(jnp.where(sides, through, along))
                by_y.append(jnp.where(sides, along, through))
            mix, keep = strip_mix[l], strip_keep[l]
            spread = [mid[c] + mix * (total[c] - 4.0 * mid[c]) for c in range(3)]
            fresh = [
                spread[0] - half * (by_x[1] + by_y[2]),
                spread[1] - half * by_x[0] + spin * mid[2],
                spread[2] - half * by_y[0] - spin * mid[1],
            ]
            open_keep = (1.0 - keep) * dry
            grown[l] = [open_keep * fresh[c] for c in range(3)]

        @pl.when(lev < 3)
        def _():
            strip_copy(r).wait_recv()

        below = [jnp.where(lev == 3, 0.0, strip_in[r, c]) for c in range(3)]
        for l in range(LEVELS - 1, -1, -1):
            below = [grown[l][c] + strip_keep[l] * below[c] for c in range(3)]
            for c in range(3):
                edges[c, l] = below[c]
        for c in range(3):
            strip_out[r, c] = below[c]

        @pl.when(lev > 0)
        def _():
            strip_copy(r).start()

        for e in range(4):
            for c in range(3):
                packed[e, c] = edges[c, :, e, :]

    def step(r, _):
        partner_copy(r).start()
        for k, d in enumerate(PLANE):
            sending[k] = packed[chosen[0, peer(d)]]
            send(r, k, d, me)

        @pl.when(r > 0)
        def _():
            for j in range(EARLY, CHUNKS):
                bulk(r - 1, j)

        settle_edges(r % 2)
        for j in range(FIRST):
            bulk(r, j)
        partner_copy(r).wait()
        theirs[...] = partner[r]
        for k, d in enumerate(PLANE):
            sending[PEERS + k] = theirs[chosen[1, peer(d)]]
            send(r, PEERS + k, d, across)
        for j in range(FIRST, EARLY):
            bulk(r, j)
        everyone = arrived.at[r, pl.ds(0, 2 * PEERS)]
        pltpu.make_async_remote_copy(
            everyone, everyone, send_sem.at[r], arrive_sem.at[r],
            device_id={"tile": across}, device_id_type=MESH,
        ).wait()
        gathered[...] = arrived[r]
        gathered[across] = theirs[chosen[1, me]]
        advance_edges(r)
        return 0

    lax.fori_loop(0, STEPS, step, 0)
    for j in range(EARLY, CHUNKS):
        bulk(STEPS - 1, j)
    settle_edges(STEPS % 2)
    store = pltpu.make_async_copy(
        state.at[STEPS % 2, :, :, pl.ds(TOP, SIDE)], out_hbm, load_sem
    )
    store.start()

    @pl.when(lev > 0)
    def _():
        def drain(r, _):
            for j in range(CHUNKS - 2, CHUNKS):
                carry_copy(r, j).wait_send()
            strip_copy(r).wait_send()
            return 0

        lax.fori_loop(0, STEPS, drain, 0)

    store.wait()


def per_device(
    adjoint_state, diffusivity, retention, coriolis,
    neighbours, edge_from, rotation, seam_length, wet_mask,
):
    tiles = neighbours.shape[0]
    f32 = jnp.float32
    vmem, dma = pltpu.VMEM, pltpu.SemaphoreType.DMA
    strips = (3, LEVELS, 4, SIDE)
    small = pl.BlockSpec(memory_space=pltpu.SMEM)
    anywhere = pl.BlockSpec(memory_space=pltpu.HBM)
    out = pl.pallas_call(
        kernel,
        out_shape=jax.ShapeDtypeStruct((3, LEVELS, SIDE, SIDE), f32),
        in_specs=[small] * 4 + [anywhere] * 5,
        out_specs=pl.BlockSpec(memory_space=pltpu.VMEM),
        scratch_shapes=[
            vmem((2, 3, LEVELS, SIDE + 2 * TOP, SIDE), f32),
            vmem((LEVELS, SIDE, SIDE), f32),
            vmem((LEVELS, SIDE, SIDE), f32),
            vmem((SIDE, SIDE), f32),
            vmem((SIDE, SIDE), jnp.int32),
            vmem((SIDE, SIDE), f32),
            vmem(strips, f32),
            vmem((4, 3, LEVELS, SIDE), f32),
            vmem(strips, f32),
            vmem(strips, f32),
            vmem(strips, f32),
            vmem(strips, f32),
            vmem((LEVELS, 4, SIDE), f32),
            vmem((LEVELS, 4, SIDE), f32),
            vmem((4, SIDE), f32),
            vmem((4, SIDE), f32),
            vmem((4, 4, SIDE), f32),
            vmem((4, 4, SIDE), f32),
            vmem((4, 4, SIDE), f32),
            vmem((4, 4, SIDE), jnp.int32),
            vmem((SIDE, SIDE), f32),
            pltpu.SMEM((2, tiles), jnp.int32),
            vmem((2 * PEERS, 3, LEVELS, SIDE), f32),
            vmem((STEPS, tiles, 3, LEVELS, SIDE), f32),
            vmem((STEPS, 4, 3, LEVELS, SIDE), f32),
            vmem((tiles, 3, LEVELS, SIDE), f32),
            vmem((4, 3, LEVELS, SIDE), f32),
            vmem((STEPS, CHUNKS, 3, ROWS, SIDE), f32),
            vmem((STEPS, CHUNKS, 3, ROWS, SIDE), f32),
            vmem((STEPS, 3, 4, SIDE), f32),
            vmem((STEPS, 3, 4, SIDE), f32),
            dma,
            dma((4,)),
            dma((STEPS,)),
            dma((STEPS,)),
            dma((STEPS,)),
            dma((STEPS,)),
            dma((STEPS, CHUNKS)),
            dma((STEPS, CHUNKS)),
            dma((STEPS,)),
            dma((STEPS,)),
        ],
        compiler_params=pltpu.CompilerParams(
            collective_id=0, has_side_effects=True, vmem_limit_bytes=60 << 20
        ),
    )(
        neighbours.T, edge_from.T, rotation.T, seam_length.T,
        adjoint_state[:, :, 0], diffusivity[:, 0], retention[:, 0], coriolis[0], wet_mask[0],
    )
    return out[:, :, None]


def solution(mesh):
    in_specs = (
        P(None, "lev", "tile", None, None),
        P("lev", "tile", None, None),
        P("lev", "tile", None, None),
        P("tile", None, None),
        P(),
        P(),
        P(),
        P(),
        P("tile", None, None),
    )
    out_specs = P(None, "lev", "tile", None, None)
    return jax.shard_map(
        per_device, mesh=mesh, in_specs=in_specs, out_specs=out_specs, check_vma=False
    )
```

```python
import functools

import jax
import jax.numpy as jnp
from jax import lax
from jax.experimental import pallas as pl
from jax.experimental.pallas import tpu as pltpu
from jax.sharding import PartitionSpec as P

STEPS = 4
COUPLING = 0.25
SIDE = 128
LEVELS = 4
PLANES = 3 * LEVELS
CHUNKS = 8
FIRST = 2
EARLY = 8
ROWS = SIDE // CHUNKS
SUB = 16
TOP = 8
MESH = pl.DeviceIdType.MESH
WEST, EAST, SOUTH, NORTH = range(4)


def distance(x, y):
    return min(x, 4 - x) + min(y, 4 - y)


PLANE = sorted(
    [(x, y, c) for x in range(4) for y in range(4) for c in range(2) if (x, y, c) != (0, 0, 0)],
    key=lambda d: (-distance(d[0], d[1]), -d[2]),
)
PEERS = len(PLANE)


def kernel(
    neighbours, edge_from, rotation, seam_length,
    state_hbm, diffusivity_hbm, retention_hbm, coriolis_hbm, wet_hbm,
    out_hbm,
    state, diffusivity, retention, coriolis, wet_mask, wet, edges, packed, inner, halo, corner_up, corner_down,
    strip_mix, strip_keep, strip_spin, strip_wet,
    turn_cos, turn_sin, inside, flips,
    columns, chosen, sending, arrived, partner, gathered, theirs, carry_out, carry_in, strip_out, strip_in,
    load_sem, coefficient_sem, send_sem, arrive_sem, partner_send, partner_arrive,
    carry_send, carry_arrive, strip_send, strip_arrive,
):
    me = lax.axis_index("tile")
    lev = lax.axis_index("lev")
    px, py, pz, pc = me // 16, (me // 4) % 4, (me // 2) % 2, me % 2
    across = ((px * 4 + py) * 2 + (1 - pz)) * 2 + pc
    down, up = (lev + 3) % 4, (lev + 1) % 4
    half = COUPLING * 0.5

    def peer(d):
        return (((px + d[0]) % 4 * 4 + (py + d[1]) % 4) * 2 + pz) * 2 + (pc + d[2]) % 2

    load = pltpu.make_async_copy(state_hbm, state.at[0, :, :, pl.ds(TOP, SIDE)], load_sem)
    loads = [
        pltpu.make_async_copy(source, target, coefficient_sem.at[i])
        for i, (source, target) in enumerate(
            [
                (diffusivity_hbm, diffusivity), (retention_hbm, retention),
                (coriolis_hbm, coriolis), (wet_hbm, wet_mask),
            ]
        )
    ]
    for copy in loads:
        copy.start()
    load.start()

    barrier = pltpu.get_barrier_semaphore()
    pl.semaphore_signal(barrier, inc=1, device_id={"tile": across}, device_id_type=MESH)
    for d in PLANE:
        pl.semaphore_signal(barrier, inc=1, device_id={"tile": peer(d)}, device_id_type=MESH)
    pl.semaphore_signal(barrier, inc=1, device_id={"lev": up}, device_id_type=MESH)
    pl.semaphore_signal(barrier, inc=1, device_id={"lev": down}, device_id_type=MESH)

    def choose(k, _):
        t = (k // 2) * 4 + pz * 2 + k % 2
        mine, theirs = jnp.int32(0), jnp.int32(0)
        for s in range(4):
            source, edge = neighbours[s, t], edge_from[s, t]
            mine = mine + jnp.where(source == me, edge, 0)
            theirs = theirs + jnp.where(source == across, edge, 0)
        chosen[0, t] = mine
        chosen[1, t] = theirs
        return 0

    lax.fori_loop(0, 32, choose, 0)

    lane4 = lax.broadcasted_iota(jnp.int32, (4, SIDE), 1)
    edge4 = lax.broadcasted_iota(jnp.int32, (4, SIDE), 0)
    lane_sub = lax.broadcasted_iota(jnp.int32, (ROWS, SIDE), 1)
    for s in range(4):
        turn = rotation[s, me]
        cells = seam_length[s, me]
        cosine = (turn == 0).astype(jnp.float32) - (turn == 2).astype(jnp.float32)
        sine = (turn == 1).astype(jnp.float32) - (turn == 3).astype(jnp.float32)
        flip = (turn == 1).astype(jnp.int32) + (turn == 2).astype(jnp.int32)
        within = jnp.where(lane4 < cells, 1.0, 0.0).astype(jnp.float32)
        inside[s] = within
        turn_cos[s] = within * cosine
        turn_sin[s] = within * sine
        flips[s] = jnp.zeros((4, SIDE), jnp.int32) + flip

    for copy in loads:
        copy.wait()
    wet[...] = wet_mask[...].astype(jnp.float32)

    def transposed(read, count, first, last):
        for b in range(CHUNKS):
            found = jnp.zeros((ROWS, SIDE), jnp.float32)
            for p in range(count):
                value = pltpu.roll(read(p, b), (2 * p - first) % SIDE, 1)
                here = (lane_sub == 2 * p) | (lane_sub == (2 * p - first + last) % SIDE)
                found = jnp.where(here, value, found)
            columns[pl.ds(b * ROWS, ROWS), :] = found
        columns[...] = columns[...].T

    def row_of(p, first, last):
        return (2 * p - first + last) % SIDE

    def coefficient(p, b):
        rows = pl.ds(b * ROWS, ROWS)
        if p < LEVELS:
            return diffusivity[p, rows, :]
        if p < 2 * LEVELS:
            return retention[p - LEVELS, rows, :]
        return coriolis[rows, :] if p == 2 * LEVELS else wet[rows, :]

    transposed(coefficient, 2 * LEVELS + 2, 0, SIDE - 1)
    for p in range(2 * LEVELS + 2):
        if p < LEVELS:
            target, source = strip_mix.at[p], diffusivity.at[p]
        elif p < 2 * LEVELS:
            target, source = strip_keep.at[p - LEVELS], retention.at[p - LEVELS]
        else:
            target, source = (strip_spin, coriolis) if p == 2 * LEVELS else (strip_wet, wet)
        target[pl.ds(WEST, 1), :] = columns[pl.ds(2 * p, 1), :]
        target[pl.ds(EAST, 1), :] = columns[pl.ds(row_of(p, 0, SIDE - 1), 1), :]
        target[pl.ds(SOUTH, 1), :] = source[pl.ds(0, 1), :]
        target[pl.ds(NORTH, 1), :] = source[pl.ds(SIDE - 1, 1), :]

    load.wait()

    def plane_rows(now):
        return lambda p, b: state[now, p // LEVELS, p % LEVELS, pl.ds(TOP + b * ROWS, ROWS), :]

    transposed(plane_rows(0), PLANES, 0, SIDE - 1)
    for p in range(PLANES):
        c, l = p // LEVELS, p % LEVELS
        edges[c, l, pl.ds(WEST, 1), :] = columns[pl.ds(2 * p, 1), :]
        edges[c, l, pl.ds(EAST, 1), :] = columns[pl.ds(row_of(p, 0, SIDE - 1), 1), :]
        edges[c, l, pl.ds(SOUTH, 1), :] = state[0, c, l, pl.ds(TOP, 1), :]
        edges[c, l, pl.ds(NORTH, 1), :] = state[0, c, l, pl.ds(TOP + SIDE - 1, 1), :]
    for e in range(4):
        for c in range(3):
            packed[e, c] = edges[c, :, e, :]

    pl.semaphore_wait(barrier, PEERS + 3)

    def settle_edges(now, last=False):
        for p in range(PLANES):
            c, l = p // LEVELS, p % LEVELS
            columns[pl.ds(2 * p, 1), :] = edges[c, l, pl.ds(WEST, 1), :]
            columns[pl.ds(row_of(p, 0, SIDE - 1), 1), :] = edges[c, l, pl.ds(EAST, 1), :]
            state[now, c, l, pl.ds(TOP, 1), :] = edges[c, l, pl.ds(SOUTH, 1), :]
            state[now, c, l, pl.ds(TOP + SIDE - 1, 1), :] = edges[c, l, pl.ds(NORTH, 1), :]
        columns[...] = columns[...].T
        for b in range(CHUNKS):
            turned = columns[pl.ds(b * ROWS, ROWS), :]
            found = jnp.zeros((ROWS, SIDE), jnp.float32)
            for p in range(PLANES):
                c, l = p // LEVELS, p % LEVELS
                rows = pl.ds(TOP + b * ROWS, ROWS)
                rim = pltpu.roll(turned, (-2 * p) % SIDE, 1)
                value = jnp.where(
                    (lane_sub == 0) | (lane_sub == SIDE - 1), rim, state[now, c, l, rows, :]
                )
                state[now, c, l, rows, :] = value
                if last:
                    continue
                here = (lane_sub == 2 * p) | (lane_sub == row_of(p, 1, SIDE - 2))
                found = jnp.where(here, pltpu.roll(value, (2 * p - 1) % SIDE, 1), found)
            if not last:
                columns[pl.ds(b * ROWS, ROWS), :] = found
        if last:
            return
        columns[...] = columns[...].T
        for p in range(PLANES):
            c, l = p // LEVELS, p % LEVELS
            inner[c, l, pl.ds(WEST, 1), :] = columns[pl.ds(2 * p, 1), :]
            inner[c, l, pl.ds(EAST, 1), :] = columns[pl.ds(row_of(p, 1, SIDE - 2), 1), :]
            inner[c, l, pl.ds(SOUTH, 1), :] = state[now, c, l, pl.ds(TOP + 1, 1), :]
            inner[c, l, pl.ds(NORTH, 1), :] = state[now, c, l, pl.ds(TOP + SIDE - 2, 1), :]

    def carry_copy(r, j):
        return pltpu.make_async_remote_copy(
            carry_out.at[r, j], carry_in.at[r, j], carry_send.at[r, j], carry_arrive.at[r, j],
            device_id={"lev": down}, device_id_type=MESH,
        )

    def strip_copy(r):
        return pltpu.make_async_remote_copy(
            strip_out.at[r], strip_in.at[r], strip_send.at[r], strip_arrive.at[r],
            device_id={"lev": down}, device_id_type=MESH,
        )

    def partner_copy(r):
        return pltpu.make_async_remote_copy(
            packed, partner.at[r], partner_send.at[r], partner_arrive.at[r],
            device_id={"tile": across}, device_id_type=MESH,
        )

    def send(r, k, d, slot):
        pltpu.make_async_remote_copy(
            sending.at[k], arrived.at[r, slot], send_sem.at[r], arrive_sem.at[r],
            device_id={"tile": peer(d)}, device_id_type=MESH,
        ).start()

    def bulk(r, j):
        now, later = r % 2, (r + 1) % 2

        @pl.when(lev < 3)
        def _():
            carry_copy(r, j).wait_recv()

        for b in range(ROWS // SUB):
            at = j * ROWS + b * SUB
            cells = pl.ds(at, SUB)
            spin, dry = coriolis[cells, :], wet[cells, :]
            below = [
                jnp.where(lev == 3, 0.0, carry_in[r, j, c, pl.ds(b * SUB, SUB), :]) for c in range(3)
            ]
            for l in range(LEVELS - 1, -1, -1):
                mid = [state[now, c, l, pl.ds(TOP + at, SUB), :] for c in range(3)]
                north = [state[now, c, l, pl.ds(TOP + at + 1, SUB), :] for c in range(3)]
                south = [state[now, c, l, pl.ds(TOP + at - 1, SUB), :] for c in range(3)]
                east = [pltpu.roll(f, SIDE - 1, 1) for f in mid]
                west = [pltpu.roll(f, 1, 1) for f in mid]
                mix, keep = diffusivity[l, cells, :], retention[l, cells, :]
                spread = [
                    mid[c] + mix * (east[c] + west[c] + north[c] + south[c] - 4.0 * mid[c])
                    for c in range(3)
                ]
                fresh = [
                    spread[0] - half * ((east[1] - west[1]) + (north[2] - south[2])),
                    spread[1] - half * (east[0] - west[0]) + spin * mid[2],
                    spread[2] - half * (north[0] - south[0]) - spin * mid[1],
                ]
                open_keep = (1.0 - keep) * dry
                below = [open_keep * fresh[c] + keep * below[c] for c in range(3)]
                for c in range(3):
                    state[later, c, l, pl.ds(TOP + at, SUB), :] = below[c]
            for c in range(3):
                carry_out[r, j, c, pl.ds(b * SUB, SUB), :] = below[c]

        @pl.when(lev > 0)
        def _():
            if j >= 2:
                @pl.when(r < STEPS - 1)
                def _():
                    carry_copy(r, j - 2).wait_send()
            carry_copy(r, j).start()

    def advance_edges(r):
        for s in range(4):
            source = neighbours[s, me]
            strip = gathered[source]
            turned = []
            for c in range(3):
                mirrored = jnp.take_along_axis(strip[c], SIDE - 1 - lane4, axis=1)
                turned.append(jnp.where(flips[s] > 0, mirrored, strip[c]))
            around = [
                turned[0] * inside[s],
                turn_cos[s] * turned[1] + turn_sin[s] * turned[2],
                turn_cos[s] * turned[2] - turn_sin[s] * turned[1],
            ]
            for c in range(3):
                halo[c, :, s, :] = around[c]
                if s == NORTH or s == EAST:
                    first = 0 if s == NORTH else 2
                    corner_up[c, :, first, :] = around[c]
                    corner_up[c, :, first + 1, :] = around[c]
                else:
                    first = 0 if s == SOUTH else 2
                    corner_down[c, :, first, :] = around[c]
                    corner_down[c, :, first + 1, :] = around[c]

        sides = edge4 < 2
        leading = (edge4 == WEST) | (edge4 == SOUTH)
        sign = jnp.where(leading, 1.0, -1.0).astype(jnp.float32)
        spin, dry = strip_spin[...], strip_wet[...]

        grown = [None] * LEVELS
        for l in range(LEVELS - 1, -1, -1):
            mid = [edges[c, l] for c in range(3)]
            total, by_x, by_y = [], [], []
            for c in range(3):
                above, beneath = corner_up[c, l], corner_down[c, l]
                far = jnp.where(leading, pltpu.roll(above, SIDE - 1, 1), above)
                near = jnp.where(leading, beneath, pltpu.roll(beneath, 1, 1))
                ahead = jnp.where(lane4 == SIDE - 1, far, pltpu.roll(mid[c], SIDE - 1, 1))
                behind = jnp.where(lane4 == 0, near, pltpu.roll(mid[c], 1, 1))
                outer, within = halo[c, l], inner[c, l]
                total.append(outer + within + ahead + behind)
                through = sign * (within - outer)
                along = ahead - behind
                by_x.append(jnp.where(sides, through, along))
                by_y.append(jnp.where(sides, along, through))
            mix, keep = strip_mix[l], strip_keep[l]
            spread = [mid[c] + mix * (total[c] - 4.0 * mid[c]) for c in range(3)]
            fresh = [
                spread[0] - half * (by_x[1] + by_y[2]),
                spread[1] - half * by_x[0] + spin * mid[2],
                spread[2] - half * by_y[0] - spin * mid[1],
            ]
            open_keep = (1.0 - keep) * dry
            grown[l] = [open_keep * fresh[c] for c in range(3)]

        @pl.when(lev < 3)
        def _():
            strip_copy(r).wait_recv()

        below = [jnp.where(lev == 3, 0.0, strip_in[r, c]) for c in range(3)]
        for l in range(LEVELS - 1, -1, -1):
            below = [grown[l][c] + strip_keep[l] * below[c] for c in range(3)]
            for c in range(3):
                edges[c, l] = below[c]
        for c in range(3):
            strip_out[r, c] = below[c]

        @pl.when(lev > 0)
        def _():
            strip_copy(r).start()

        for e in range(4):
            for c in range(3):
                packed[e, c] = edges[c, :, e, :]

    def step(r, _):
        partner_copy(r).start()
        for k, d in enumerate(PLANE):
            sending[k] = packed[chosen[0, peer(d)]]
            send(r, k, d, me)

        @pl.when(r > 0)
        def _():
            for j in range(EARLY, CHUNKS):
                bulk(r - 1, j)

        settle_edges(r % 2)
        for j in range(FIRST):
            bulk(r, j)
        partner_copy(r).wait()
        theirs[...] = partner[r]
        for k, d in enumerate(PLANE):
            sending[PEERS + k] = theirs[chosen[1, peer(d)]]
            send(r, PEERS + k, d, across)
        for j in range(FIRST, EARLY):
            bulk(r, j)
        everyone = arrived.at[r, pl.ds(0, 2 * PEERS)]
        pltpu.make_async_remote_copy(
            everyone, everyone, send_sem.at[r], arrive_sem.at[r],
            device_id={"tile": across}, device_id_type=MESH,
        ).wait()
        gathered[...] = arrived[r]
        gathered[across] = theirs[chosen[1, me]]
        advance_edges(r)
        return 0

    lax.fori_loop(0, STEPS, step, 0)
    for j in range(EARLY, CHUNKS):
        bulk(STEPS - 1, j)
    settle_edges(STEPS % 2, last=True)
    store = pltpu.make_async_copy(
        state.at[STEPS % 2, :, :, pl.ds(TOP, SIDE)], out_hbm, load_sem
    )
    store.start()

    @pl.when(lev > 0)
    def _():
        def drain(r, _):
            for j in range(CHUNKS - 2, CHUNKS):
                carry_copy(r, j).wait_send()
            strip_copy(r).wait_send()
            return 0

        lax.fori_loop(0, STEPS, drain, 0)
        for j in range(CHUNKS - 2):
            carry_copy(STEPS - 1, j).wait_send()

    store.wait()


def per_device(
    adjoint_state, diffusivity, retention, coriolis,
    neighbours, edge_from, rotation, seam_length, wet_mask,
):
    tiles = neighbours.shape[0]
    f32 = jnp.float32
    vmem, dma = pltpu.VMEM, pltpu.SemaphoreType.DMA
    strips = (3, LEVELS, 4, SIDE)
    small = pl.BlockSpec(memory_space=pltpu.SMEM)
    anywhere = pl.BlockSpec(memory_space=pltpu.HBM)
    out = pl.pallas_call(
        kernel,
        out_shape=jax.ShapeDtypeStruct((3, LEVELS, SIDE, SIDE), f32),
        in_specs=[small] * 4 + [anywhere] * 5,
        out_specs=pl.BlockSpec(memory_space=pltpu.VMEM),
        scratch_shapes=[
            vmem((2, 3, LEVELS, SIDE + 2 * TOP, SIDE), f32),
            vmem((LEVELS, SIDE, SIDE), f32),
            vmem((LEVELS, SIDE, SIDE), f32),
            vmem((SIDE, SIDE), f32),
            vmem((SIDE, SIDE), jnp.int32),
            vmem((SIDE, SIDE), f32),
            vmem(strips, f32),
            vmem((4, 3, LEVELS, SIDE), f32),
            vmem(strips, f32),
            vmem(strips, f32),
            vmem(strips, f32),
            vmem(strips, f32),
            vmem((LEVELS, 4, SIDE), f32),
            vmem((LEVELS, 4, SIDE), f32),
            vmem((4, SIDE), f32),
            vmem((4, SIDE), f32),
            vmem((4, 4, SIDE), f32),
            vmem((4, 4, SIDE), f32),
            vmem((4, 4, SIDE), f32),
            vmem((4, 4, SIDE), jnp.int32),
            vmem((SIDE, SIDE), f32),
            pltpu.SMEM((2, tiles), jnp.int32),
            vmem((2 * PEERS, 3, LEVELS, SIDE), f32),
            vmem((STEPS, tiles, 3, LEVELS, SIDE), f32),
            vmem((STEPS, 4, 3, LEVELS, SIDE), f32),
            vmem((tiles, 3, LEVELS, SIDE), f32),
            vmem((4, 3, LEVELS, SIDE), f32),
            vmem((STEPS, CHUNKS, 3, ROWS, SIDE), f32),
            vmem((STEPS, CHUNKS, 3, ROWS, SIDE), f32),
            vmem((STEPS, 3, 4, SIDE), f32),
            vmem((STEPS, 3, 4, SIDE), f32),
            dma,
            dma((4,)),
            dma((STEPS,)),
            dma((STEPS,)),
            dma((STEPS,)),
            dma((STEPS,)),
            dma((STEPS, CHUNKS)),
            dma((STEPS, CHUNKS)),
            dma((STEPS,)),
            dma((STEPS,)),
        ],
        compiler_params=pltpu.CompilerParams(
            collective_id=0, has_side_effects=True, vmem_limit_bytes=60 << 20
        ),
    )(
        neighbours.T, edge_from.T, rotation.T, seam_length.T,
        adjoint_state[:, :, 0], diffusivity[:, 0], retention[:, 0], coriolis[0], wet_mask[0],
    )
    return out[:, :, None]


def solution(mesh):
    in_specs = (
        P(None, "lev", "tile", None, None),
        P("lev", "tile", None, None),
        P("lev", "tile", None, None),
        P("tile", None, None),
        P(),
        P(),
        P(),
        P(),
        P("tile", None, None),
    )
    out_specs = P(None, "lev", "tile", None, None)
    return jax.shard_map(
        per_device, mesh=mesh, in_specs=in_specs, out_specs=out_specs, check_vma=False
    )
```
